128 devices in a mesh: row: 8 (over z, core), col: 16 (over y, x).
Axes of the slice: x: 4, y: 4, z: 4, core: 2. Of those that a mesh axis runs over, the one named last changes fastest.
Arguments:
- front_matrix: float32 [16384, 16384], P('row', 'col'), may hold values from -6 to 6
- child_tiles: float32 [8, 16, 16, 256, 256], P('row', 'col'), may hold values from -6 to 6
- target_column: int32 [8, 16, 16, 1], P('row', 'col'), may hold values from 0 to 15; in each aligned block of 16 rows (0 to 15, 16 to 31, ..., all dimensions but the last counted through in order) at most 2 rows name the same one
- target_tile: int32 [8, 16, 16], P('row', 'col'), may hold values from 0 to 31
- row_map: int32 [8, 16, 16, 256], P('row', 'col'), may hold values from 0 to 255, each once within a row
- col_map: int32 [8, 16, 16, 256], P('row', 'col'), may hold values from 0 to 255, each once within a row
- pivot_inverse: float32 [2, 256, 256], replicated, may hold values from -0.025 to 0.15
Outputs:
- front_out: float32 [16384, 16384], P('row', 'col')
The draws below stay inside these ranges and needn't reach their ends.
Inputs may be any that keep to these rules, and one draw needn't show every extreme that they name: `target_column`: each device sends at most 2 of its tiles to one device column, and some device sends exactly 2 to one column.
All inputs are finite; a program needn't handle non-finite values.
Results may differ from the reference program's by a relative error of at most 0.0003.
Values sent between devices are 32-bit elements; how exact they have to be, the bound alone decides.
A program may use at most 128 MiB of HBM per device.

```python
import math
import jax
import jax.numpy as jnp
import numpy as np
from jax import lax

ORDER = 16384
TILE = 256
PANELS = 2
CT = 16
CAP = 2
TRD = 8
TCD = 4
N_ROW = 8
N_COL = 16


def draw_pivot_inverse(key, part):
    first_key, second_key = jax.random.split(key, 2)
    diagonal = jax.random.uniform(first_key, (PANELS, TILE), jnp.float32, 1.0, 2.0)
    normal_draw = jnp.clip(jax.random.normal(second_key, (PANELS, TILE, TILE), jnp.float32), -4.0, 4.0)
    symmetric = (normal_draw + jnp.swapaxes(normal_draw, 1, 2)) * (0.06 / 1.4142135)
    identity = jnp.eye(TILE, dtype=jnp.float32)
    return ((identity[None, :, :] * diagonal[:, :, None] + symmetric) / 16.0).astype(jnp.float32)


def set_ends(array, stream_key, low, high):
    index_at = [jax.random.randint(jax.random.fold_in(stream_key, axis), (), 0, length) for axis, length in enumerate(array.shape)]
    widest = array.shape.index(max(array.shape))
    beside = index_at[:widest] + [(index_at[widest] + 1) % array.shape[widest]] + index_at[widest + 1:]
    return array.at[tuple(index_at)].set(low).at[tuple(beside)].set(high)


def steps_of(key, extent, cuts, least, high):
    factor_of = 1.0
    for position, shards_of in cuts:
        draws = jax.random.uniform(jax.random.fold_in(jax.random.fold_in(key, 6), position), (shards_of,), jnp.float32, least / len(cuts), high / len(cuts))
        factor_of = factor_of * jnp.repeat(jnp.exp(draws), extent[position] // shards_of).reshape((-1,) + (1,) * (len(extent) - 1 - position))
    return factor_of


def routed_block(own_key, own, number, rows, amount, top, bound, slope):
    sequence = jax.random.permutation(own_key, amount)
    heavy_load, common = portions_of(amount, rows * top, bound, slope, True), portions_of(amount, rows * top, bound, slope, False)
    places = jnp.arange(amount)

    def named(sizes, turn):
        used = int((sizes > 0).sum())
        fixed = max(1, used // 4)
        passed = fixed + (places - fixed + turn * (used - fixed)) % max(1, amount - fixed)
        return jnp.zeros((amount,), jnp.int32).at[sequence[jnp.where(places < fixed, places, passed)]].set(jnp.asarray(sizes, jnp.int32))

    sizes = jnp.where(number % 4 == 0, named(heavy_load, number // 4), named(common, number - number // 4 - 1))
    mixed = jax.random.permutation(jax.random.fold_in(own, 3), amount)
    giver, taker = mixed[0:amount // 2 * 2:2], mixed[1:amount // 2 * 2:2]
    room = jnp.minimum(sizes[giver] - 1, bound - sizes[taker]) // 2
    room = jnp.where((giver == sequence[0]) | (taker == sequence[0]) | (sizes[taker] == 0), 0, jnp.maximum(room, 0))
    passed = jax.random.randint(jax.random.fold_in(own, 4), (amount // 2,), 0, 1 << 20) % (room + 1)
    sizes = sizes.at[giver].add(-passed).at[taker].add(passed)
    members = jnp.searchsorted(jnp.cumsum(sizes), jnp.arange(rows * top), side="right").astype(jnp.int32)
    listing = members.reshape(top, rows).T
    listing = listing[jax.random.permutation(jax.random.fold_in(own, 1), rows)]
    turn = jax.random.randint(jax.random.fold_in(own, 2), (rows, 1), 0, top)
    return jnp.take_along_axis(listing, (jnp.arange(top)[None, :] + turn) % top, axis=1)


def portions_of(number_of, total, bound, slope, full):
    weights = [(1 << 20) // math.isqrt(rank ** slope) + 1 for rank in range(1, number_of + 1)]
    largest = bound if full else min(bound, max(-(-total // number_of), total * weights[0] // sum(weights)))
    least = 1 if total - largest >= number_of - 1 else 0
    given, rest = [largest] + [least] * (number_of - 1), total - largest - least * (number_of - 1)
    while rest > 0:
        movable = [i for i in range(1, number_of) if given[i] < largest] or [i for i in range(1, number_of) if given[i] < bound]
        whole, left = sum([weights[i] for i in movable]), rest
        for i in movable:
            extra = min(bound - given[i], max(1, left * weights[i] // whole), rest)
            given[i] = given[i] + extra
            rest = rest - extra
    return np.array(given)


def centred(key, shape, scale, bound, shards=(), kind=jnp.bfloat16):
    values = jax.random.normal(key, shape, jnp.float32) * scale
    if len(shards) > 0:
        values = steps_of(key, shape, shards, -0.22, 0.18) * values
    return jnp.clip(values, min=-bound, max=bound).astype(kind)


def setup_inputs(seed: int = 0) -> dict:
    key_list = jax.random.split(jax.random.key(seed), 8)
    front_matrix = centred(key_list[0], (ORDER, ORDER), 1.0, 6.0, ((0, 8), (1, 16)), jnp.float32)
    child_tiles = centred(key_list[1], (N_ROW, N_COL, CT, TILE, TILE), 1.0, 6.0, ((0, 8), (1, 16)), jnp.float32)
    target_column_keys = jax.random.split(jax.random.fold_in(key_list[2], 1), N_ROW * N_COL * CT // CT)
    target_column_turns = jax.random.permutation(jax.random.fold_in(key_list[2], 3), N_ROW * N_COL * CT // CT)
    target_column = jax.vmap(lambda own, number: routed_block(jax.random.fold_in(key_list[2], 2), own, number, CT, N_COL, 1, CAP, 2))(target_column_keys, target_column_turns).reshape((N_ROW, N_COL, CT, 1))
    target_tile = set_ends(jax.random.randint(key_list[3], (N_ROW, N_COL, CT), 0, TRD * TCD), jax.random.fold_in(key_list[3], 1), 0, (TRD * TCD) - 1).astype(jnp.int32)
    row_map = jax.vmap(lambda own: jax.random.permutation(own, TILE))(jax.random.split(key_list[4], N_ROW * N_COL * CT)).reshape((N_ROW, N_COL, CT, TILE)).astype(jnp.int32)
    col_map = jax.vmap(lambda own: jax.random.permutation(own, TILE))(jax.random.split(key_list[5], N_ROW * N_COL * CT)).reshape((N_ROW, N_COL, CT, TILE)).astype(jnp.int32)
    pivot_inverse = draw_pivot_inverse(jax.random.fold_in(key_list[7], 71), 0)
    return dict(front_matrix=front_matrix, child_tiles=child_tiles, target_column=target_column, target_tile=target_tile, row_map=row_map, col_map=col_map, pivot_inverse=pivot_inverse)


def reference(front_matrix, child_tiles, target_column, target_tile, row_map, col_map, pivot_inverse):
    tile_size = child_tiles.shape[-1]
    row_count = child_tiles.shape[0]
    col_count = child_tiles.shape[1]
    tile_count = child_tiles.shape[2]
    block_rows = front_matrix.shape[0] // row_count
    block_cols = front_matrix.shape[1] // col_count
    tile_cols = block_cols // tile_size
    sources = row_count * col_count
    source_row = jnp.arange(sources, dtype=jnp.int32) // col_count
    source_items = (
        child_tiles.reshape(sources, tile_count, tile_size, tile_size),
        target_column.reshape(sources, tile_count).astype(jnp.int32),
        target_tile.reshape(sources, tile_count).astype(jnp.int32),
        row_map.reshape(sources, tile_count, tile_size).astype(jnp.int32),
        col_map.reshape(sources, tile_count, tile_size).astype(jnp.int32),
        source_row,
    )

    def add_source(matrix, entries):
        child_block, columns, places, row_maps, col_maps, source_band = entries
        row_index = source_band * block_rows + (places // tile_cols)[:, None] * tile_size + row_maps
        col_index = columns[:, None] * block_cols + (places % tile_cols)[:, None] * tile_size + col_maps
        matrix = matrix.at[row_index[:, :, None], col_index[:, None, :]].add(child_block)
        return matrix, None

    matrix, unused_out = lax.scan(add_source, front_matrix, source_items)
    for panel_index in range(PANELS):
        begin = panel_index * tile_size
        finish = begin + tile_size
        lower = jnp.dot(matrix[finish:, begin:finish], pivot_inverse[panel_index], precision=lax.Precision.HIGHEST)
        update = jnp.dot(lower, matrix[begin:finish, finish:], precision=lax.Precision.HIGHEST)
        matrix = matrix.at[finish:, finish:].set(matrix[finish:, finish:] - update)
        matrix = matrix.at[finish:, begin:finish].set(lower)
    return matrix
```

```python
import functools
import jax
import jax.numpy as jnp
from jax import lax
from jax.experimental import pallas as pl
from jax.experimental.pallas import tpu as pltpu
from jax.sharding import PartitionSpec as P

TILE = 256
SLOT = TILE + 8
CAP = 2
N_ROW = 8
N_COL = 16
MESH = pl.DeviceIdType.MESH
DMA = pltpu.SemaphoreType.DMA
ANY = pl.BlockSpec(memory_space=pl.ANY)


def halves(value):
    high = value.astype(jnp.bfloat16)
    low = (value - high.astype(jnp.float32)).astype(jnp.bfloat16)
    return high, low


def product(left, right, dims=(((1,), (0,)), ((), ()))):
    return lax.dot_general(left, right, dims, preferred_element_type=jnp.float32)


def product3(left, right):
    left_high, left_low = left
    right_high, right_low = right
    return (
        product(left_high, right_high)
        + product(left_high, right_low)
        + product(left_low, right_high)
    )


def permute_kernel(source, mark, tile, row_map, col_map, out):
    slot = pl.program_id(0)

    @pl.when(mark[slot] >= 0)
    def _():
        order = lax.broadcasted_iota(jnp.int32, (TILE, TILE), 0)
        to_row = (order == row_map[0]).astype(jnp.bfloat16)
        to_col = (order == col_map[0]).astype(jnp.bfloat16)
        across = (((1,), (1,)), ((), ()))
        result = None
        for part in halves(tile[0]):
            moved = product(part, to_col, across).astype(jnp.bfloat16)
            moved = product(to_row, moved)
            result = moved if result is None else result + moved
        out[0, :TILE, :] = result

    out[0, TILE:, :] = jnp.full((8, TILE), mark[slot].astype(jnp.float32))


def permute(source, mark, tiles, row_map, col_map):
    slots = source.shape[0]
    count = tiles.shape[0]
    return pl.pallas_call(
        permute_kernel,
        out_shape=jax.ShapeDtypeStruct((slots, SLOT, TILE), jnp.float32),
        grid_spec=pltpu.PrefetchScalarGridSpec(
            num_scalar_prefetch=2,
            grid=(slots,),
            in_specs=[
                pl.BlockSpec((1, TILE, TILE), lambda s, src, mk: (src[s], 0, 0)),
                pl.BlockSpec((1, 1, TILE), lambda s, src, mk: (src[s], 0, 0)),
                pl.BlockSpec((1, 1, TILE), lambda s, src, mk: (src[s], 0, 0)),
            ],
            out_specs=pl.BlockSpec((1, SLOT, TILE), lambda s, src, mk: (s, 0, 0)),
        ),
        name="permute",
    )(source, mark, tiles, row_map.reshape(count, 1, TILE), col_map.reshape(count, 1, TILE))


NEAR = [(1, 0), (3, 0), (0, 1), (0, 3), (1, 1), (3, 3), (1, 3), (3, 1)]
FAR = [(2, 0), (0, 2), (2, 2), (2, 1), (2, 3), (1, 2), (3, 2)]


def cut(rows, parts):
    edges = [rows // 8 * i // parts * 8 for i in range(parts + 1)]
    return [(edges[i], edges[i + 1] - edges[i]) for i in range(parts)]


def exchange_kernel(sent, got, relay, own_sem, s1, r1, s2, r2, s3, r3):
    row = lax.axis_index("row")
    col = lax.axis_index("col")
    y, x = col // 4, col % 4
    rows = sent.shape[1]

    def at(dx, dy):
        return (y + dy) % 4 * 4 + (x + dx) % 4

    barrier = pltpu.get_barrier_semaphore()
    for offset in NEAR:
        pl.semaphore_signal(barrier, inc=1, device_id=(row, at(*offset)), device_id_type=MESH)
    pl.semaphore_wait(barrier, len(NEAR))
    own = pltpu.make_async_copy(sent.at[col], got.at[col], own_sem)
    own.start()
    legs = []
    for i, (dx, dy) in enumerate(FAR):
        for half, (first, count) in enumerate(cut(rows, 2)):
            step = 1 if half == 0 else 3
            rx, ry = (step if dx == 2 else 0), (step if dy == 2 else 0)
            j = 2 * i + half
            leg = pltpu.make_async_remote_copy(
                src_ref=sent.at[at(dx, dy), pl.ds(first, count)],
                dst_ref=relay.at[j, pl.ds(0, count)],
                send_sem=s2.at[j],
                recv_sem=r2.at[j],
                device_id=(row, at(rx, ry)),
                device_id_type=MESH,
            )
            leg.start()
            legs.append((leg, j, at(-rx, -ry), at(dx - rx, dy - ry), first, count))
    straight = []
    for i, (dx, dy) in enumerate(NEAR):
        copy = pltpu.make_async_remote_copy(
            src_ref=sent.at[at(dx, dy)],
            dst_ref=got.at[col],
            send_sem=s1.at[i],
            recv_sem=r1.at[i],
            device_id=(row, at(dx, dy)),
            device_id_type=MESH,
        )
        straight.append(copy)
    for copy in straight[:4]:
        copy.start()
    onward = []
    for leg, j, origin, target, first, count in legs:
        leg.wait_recv()
        copy = pltpu.make_async_remote_copy(
            src_ref=relay.at[j, pl.ds(0, count)],
            dst_ref=got.at[origin, pl.ds(first, count)],
            send_sem=s3.at[j],
            recv_sem=r3.at[j],
            device_id=(row, target),
            device_id_type=MESH,
        )
        copy.start()
        onward.append(copy)
    for copy in straight[4:]:
        copy.start()
    for copy in straight + onward:
        copy.wait()
    for leg, *_ in legs:
        leg.wait_send()
    own.wait()


def exchange(sent):
    rows = sent.shape[1]
    return pl.pallas_call(
        exchange_kernel,
        out_shape=jax.ShapeDtypeStruct(sent.shape, jnp.float32),
        in_specs=[ANY],
        out_specs=ANY,
        scratch_shapes=[pltpu.VMEM((2 * len(FAR), cut(rows, 2)[1][1], TILE), jnp.float32), DMA]
        + [DMA((len(NEAR),))] * 2
        + [DMA((2 * len(FAR),))] * 4,
        compiler_params=pltpu.CompilerParams(collective_id=1, has_side_effects=True),
        name="exchange",
    )(sent)


def assemble_kernel(target, front, got, out):
    band = pl.program_id(0)
    out[...] = front[...]
    for slot in range(target.shape[0]):
        place = target[slot]

        @pl.when((place >= 0) & (place // 4 == band))
        def _():
            lanes = pl.ds(pl.multiple_of(place % 4 * TILE, TILE), TILE)
            out[:, lanes] += got[slot // CAP, pl.ds(slot % CAP * SLOT, TILE), :]


def assemble(target, front, got):
    rows, cols = front.shape
    return pl.pallas_call(
        assemble_kernel,
        out_shape=jax.ShapeDtypeStruct(front.shape, jnp.float32),
        grid_spec=pltpu.PrefetchScalarGridSpec(
            num_scalar_prefetch=1,
            grid=(rows // TILE,),
            in_specs=[
                pl.BlockSpec((TILE, cols), lambda i, t: (i, 0)),
                pl.BlockSpec(got.shape, lambda i, t: (0, 0, 0), pipeline_mode=pl.Buffered(1)),
            ],
            out_specs=pl.BlockSpec((TILE, cols), lambda i, t: (i, 0)),
        ),
        name="assemble",
    )(target, front, got)


PIECE = 32
PIECES = 16
BAND = 16
CORNER_AT = 10


def spanning_trees():
    trees = []
    for tree in range(4):
        depth, edges = {}, []

        def grow(node, last, level):
            depth[node] = level
            for turn in range(last + 1, 4):
                bit = ((turn + 1) % 4 + tree) % 4
                child = node ^ (1 << bit)
                if child != 0:
                    edges.append((node, bit))
                    grow(child, turn, level + 1)

        grow(1 << tree, -1, 1)
        edges.append((0, tree))
        trees.append((depth, edges))
    return trees


def gray(column):
    y, x = column // 4, column % 4
    return (x ^ (x >> 1)) + 4 * (y ^ (y >> 1))


def panel_kernel(front, block, band, corner, ts, tr, cs, cr, us, ur, qs, qr, vs, vr, ws, wr):
    row = lax.axis_index("row")
    col = lax.axis_index("col")
    y, x = col // 4, col % 4
    z, core = row // 2, row % 2
    beside = [
        (row, y * 4 + (x + 1 - 2 * (x % 2))),
        (row, y * 4 + 3 - x),
        (row, (y + 1 - 2 * (y % 2)) * 4 + x),
        (row, (3 - y) * 4 + x),
    ]
    along = [((z + 1) % 4 * 2 + core, col), ((z + 3) % 4 * 2 + core, col)]
    partner = (z * 2 + 1 - core, col)
    barrier = pltpu.get_barrier_semaphore()
    for device in beside + along + [partner]:
        pl.semaphore_signal(barrier, inc=1, device_id=device, device_id_type=MESH)
    pl.semaphore_wait(barrier, 7)

    trees = spanning_trees()
    names = {gray(column): column for column in range(N_COL)}
    level, sends = [], []
    for depth, edges in trees:
        at = jnp.int32(0)
        for node, steps in depth.items():
            at = at + jnp.where(col == names[node], steps, 0)
        level.append(at)
        by_bit = {}
        for bit in range(4):
            nodes = [names[node] for node, b in edges if b == bit and node != 0]
            if nodes:
                by_bit[bit] = functools.reduce(jnp.logical_or, [col == node for node in nodes])
        sends.append(by_bit)
    root = col == 0
    upper = row == 0
    leads = core == 0
    way = [z, (4 - z) % 4]

    def remote(source, target, send, receive, device):
        return pltpu.make_async_remote_copy(
            src_ref=source,
            dst_ref=target,
            send_sem=send,
            recv_sem=receive,
            device_id=device,
            device_id_type=MESH,
        )

    def block_piece(tree, piece):
        return block.at[pl.ds(pl.multiple_of((piece * 4 + tree) * PIECE, PIECE), PIECE)]

    def block_copy(tree, bit, piece, source):
        return remote(
            source, block_piece(tree, piece), ts.at[tree, bit], tr.at[tree, piece], beside[bit]
        )

    def corner_copy(tree, bit, source):
        target = corner.at[pl.ds(tree * 64, 64)]
        return remote(source, target, cs.at[tree, bit], cr.at[tree], beside[bit])

    def front_piece(tree, piece):
        first = pl.multiple_of((piece * 4 + tree) * PIECE, PIECE)
        return front.at[pl.ds(first, PIECE), pl.ds(0, 2 * TILE)]

    def band_piece(ref, half, piece):
        return ref.at[pl.ds(pl.multiple_of(half * TILE + piece * BAND, BAND), BAND)]

    def corner_half(half):
        return corner.at[pl.ds(half * TILE, TILE)]

    def step(now, carry):
        for tree in range(4):
            piece = now - level[tree] - 1

            @pl.when((piece == -1) & upper)
            def _():
                @pl.when(root)
                def _():
                    source = front.at[pl.ds(tree * 64, 64), pl.ds(TILE, TILE)]
                    corner_copy(tree, tree, source).start()

                @pl.when(jnp.logical_not(root))
                def _():
                    source = corner.at[pl.ds(tree * 64, 64)]
                    corner_copy(tree, 0, source).wait_recv()
                    for bit, here in sends[tree].items():

                        @pl.when(here)
                        def _():
                            corner_copy(tree, bit, source).start()

            @pl.when((piece >= 0) & (piece < PIECES))
            def _():
                @pl.when(root)
                def _():
                    block_copy(tree, tree, piece, front_piece(tree, piece)).start()

                @pl.when(jnp.logical_not(root))
                def _():
                    source = block_piece(tree, piece)
                    block_copy(tree, 0, piece, source).wait_recv()
                    for bit, here in sends[tree].items():

                        @pl.when(here)
                        def _():
                            block_copy(tree, bit, piece, source).start()

        for half in range(2):
            hops = way[half]
            piece = now - hops

            def band_copy(source, which):
                target = band_piece(band, half, piece)
                if which == 0:
                    return remote(source, target, us.at[half], ur.at[half, piece], along[half])
                return remote(source, target, qs.at[half], qr.at[half], partner)

            @pl.when(leads & (piece >= 0) & (piece < PIECES))
            def _():
                @pl.when(hops == 0)
                def _():
                    source = band_piece(front, half, piece)
                    band_copy(source, 0).start()
                    band_copy(source, 1).start()

                @pl.when(hops > 0)
                def _():
                    source = band_piece(band, half, piece)
                    band_copy(source, 0).wait_recv()

                    @pl.when(hops < 3)
                    def _():
                        band_copy(source, 0).start()

                    band_copy(source, 1).start()

            def pass_on(source):
                @pl.when(hops < 3)
                def _():
                    remote(source, corner_half(half), vs.at[half], vr.at[half], along[half]).start()

                remote(source, corner_half(half), ws.at[half], wr.at[half], partner).start()

            @pl.when(leads & (now == CORNER_AT + 3 * hops))
            def _():
                @pl.when(upper & root)
                def _():
                    if half == 0:
                        pass_on(front.at[pl.ds(0, TILE), pl.ds(TILE, TILE)])
                    else:
                        pass_on(front.at[pl.ds(TILE, TILE), pl.ds(0, TILE)])

                @pl.when(upper & jnp.logical_not(root))
                def _():
                    if half == 0:
                        pass_on(corner_half(0))
                    else:
                        pass_on(block.at[pl.ds(TILE, TILE), pl.ds(0, TILE)])

                @pl.when(jnp.logical_not(upper))
                def _():
                    source = corner_half(half)
                    remote(source, source, vs.at[half], vr.at[half], along[half]).wait_recv()
                    pass_on(source)

        return carry

    lax.fori_loop(0, PIECES + 6, step, 0)

    whole = block.at[pl.ds(0, PIECE * PIECES)]
    for tree in range(4):

        def sent(bit):
            remote(whole, whole, ts.at[tree, bit], tr.at[tree, 0], beside[bit]).wait_send()

            @pl.when(upper)
            def _():
                corner_copy(tree, bit, corner.at[pl.ds(tree * 64, 64)]).wait_send()

        @pl.when(root)
        def _():
            sent(tree)

        for bit, here in sends[tree].items():

            @pl.when(here)
            def _():
                sent(bit)

    for half in range(2):
        whole_band = band.at[pl.ds(half * TILE, TILE)]
        band_along = remote(whole_band, whole_band, us.at[half], ur.at[half, 0], along[half])
        band_beside = remote(whole_band, whole_band, qs.at[half], qr.at[half], partner)
        ends = corner_half(half)
        corner_along = remote(ends, ends, vs.at[half], vr.at[half], along[half])
        corner_beside = remote(ends, ends, ws.at[half], wr.at[half], partner)

        @pl.when(leads)
        def _():
            @pl.when(way[half] < 3)
            def _():
                band_along.wait_send()
                corner_along.wait_send()

            band_beside.wait_send()
            corner_beside.wait_send()

        @pl.when(jnp.logical_not(leads))
        def _():
            band_beside.wait_recv()
            corner_beside.wait_recv()


def share_panels(front):
    rows, cols = front.shape
    return pl.pallas_call(
        panel_kernel,
        out_shape=(
            jax.ShapeDtypeStruct((rows, 2 * TILE), jnp.float32),
            jax.ShapeDtypeStruct((2 * TILE, cols), jnp.float32),
            jax.ShapeDtypeStruct((2 * TILE, TILE), jnp.float32),
        ),
        in_specs=[ANY],
        out_specs=(ANY,) * 3,
        scratch_shapes=[
            DMA((4, 4)),
            DMA((4, PIECES)),
            DMA((4, 4)),
            DMA((4,)),
            DMA((2,)),
            DMA((2, PIECES)),
        ]
        + [DMA((2,))] * 6,
        compiler_params=pltpu.CompilerParams(collective_id=2, has_side_effects=True),
        name="share_panels",
    )(front)


def update_kernel(
    front, block, band, corner, top, side, inverse, out, up_high, up_low, small_high, small_low
):
    step = pl.program_id(0)
    row = lax.axis_index("row")
    root = lax.axis_index("col") == 0
    upper = row == 0

    @pl.when(step == 0)
    def _():
        band_now = jnp.where(upper, top[...], band[...])
        right = jnp.where(upper & root, top[:TILE, TILE : 2 * TILE], corner[:TILE])
        below = jnp.where(root, top[TILE:, :TILE], side[...])
        below = jnp.where(upper, below, corner[TILE:])
        for place, value in enumerate((inverse[0], inverse[1], right)):
            small_high[place], small_low[place] = halves(value)
        first = band_now[:TILE]
        first_parts = halves(first)
        ratio = product3(halves(below), (small_high[0], small_low[0]))
        second = band_now[TILE:] - product3(halves(ratio), first_parts)
        up_high[:TILE], up_low[:TILE] = first_parts
        up_high[TILE:], up_low[TILE:] = halves(second)

    current = front[...]
    columns = jnp.where(root, current[:, : 2 * TILE], block[...])
    lower_0 = product3(halves(columns[:, :TILE]), (small_high[0], small_low[0]))
    lower_0_parts = halves(lower_0)
    rest = columns[:, TILE:] - product3(lower_0_parts, (small_high[2], small_low[2]))
    lower_1 = product3(halves(rest), (small_high[1], small_low[1]))
    number = row * (N_ROW * TILE // TILE) + step
    live_0 = number >= 1
    live_1 = number >= 2
    both = jnp.concatenate(
        [jnp.where(live_0, lower_0, 0.0), jnp.where(live_1, lower_1, 0.0)], axis=1
    )
    high, low = halves(both)
    update = product3((high, low), (up_high[...], up_low[...]))
    out[...] = current - update

    @pl.when(root & live_0)
    def _():
        out[:, :TILE] = lower_0

    @pl.when(root & live_1)
    def _():
        out[:, TILE : 2 * TILE] = lower_1


def update(front, block, band, corner, inverse):
    rows, cols = front.shape
    once = pl.Buffered(1)
    return pl.pallas_call(
        update_kernel,
        out_shape=jax.ShapeDtypeStruct(front.shape, jnp.float32),
        grid=(rows // TILE,),
        in_specs=[
            pl.BlockSpec((TILE, cols), lambda i: (i, 0)),
            pl.BlockSpec((TILE, 2 * TILE), lambda i: (i, 0)),
            pl.BlockSpec((2 * TILE, cols), lambda i: (0, 0), pipeline_mode=once),
            pl.BlockSpec((2 * TILE, TILE), lambda i: (0, 0), pipeline_mode=once),
            pl.BlockSpec((2 * TILE, cols), lambda i: (0, 0), pipeline_mode=once),
            pl.BlockSpec((TILE, TILE), lambda i: (1, 0), pipeline_mode=once),
            pl.BlockSpec((2, TILE, TILE), lambda i: (0, 0, 0), pipeline_mode=once),
        ],
        out_specs=pl.BlockSpec((TILE, cols), lambda i: (i, 0)),
        scratch_shapes=[pltpu.VMEM((2 * TILE, cols), jnp.bfloat16)] * 2
        + [pltpu.VMEM((3, TILE, TILE), jnp.bfloat16)] * 2,
        name="update",
    )(front, block, band, corner, front, block, inverse)


def per_device(
    front_matrix, child_tiles, target_column, target_tile, row_map, col_map, pivot_inverse
):
    count = child_tiles.shape[2]
    targets = target_column.reshape(count)
    numbers = jnp.arange(count, dtype=jnp.int32)
    earlier = (targets[:, None] == targets[None, :]) & (numbers[None, :] < numbers[:, None])
    placed = targets * CAP + jnp.sum(earlier.astype(jnp.int32), axis=1)
    slots = jnp.arange(N_COL * CAP, dtype=jnp.int32)
    match = placed[None, :] == slots[:, None]
    source = jnp.sum(jnp.where(match, numbers[None, :], 0), axis=1)
    mark = jnp.sum(jnp.where(match, target_tile.reshape(1, count) + 1, 0), axis=1) - 1
    sent = permute(
        source,
        mark,
        child_tiles.reshape(count, TILE, TILE),
        row_map.reshape(count, TILE),
        col_map.reshape(count, TILE),
    )
    got = exchange(sent.reshape(N_COL, CAP * SLOT, TILE))
    target = got.reshape(N_COL * CAP, SLOT, TILE)[:, TILE, 0].astype(jnp.int32)
    front = assemble(target, front_matrix, got)
    block, band, corner = share_panels(front)
    return update(front, block, band, corner, pivot_inverse)


def solution(mesh):
    in_specs = (
        P("row", "col"),
        P("row", "col", None, None, None),
        P("row", "col", None, None),
        P("row", "col", None),
        P("row", "col", None, None),
        P("row", "col", None, None),
        P(),
    )
    return jax.shard_map(
        per_device, mesh=mesh, in_specs=in_specs, out_specs=P("row", "col"), check_vma=False
    )
```

```python
import functools
import jax
import jax.numpy as jnp
from jax import lax
from jax.experimental import pallas as pl
from jax.experimental.pallas import tpu as pltpu
from jax.sharding import PartitionSpec as P

TILE = 256
SLOT = TILE + 8
N_ROW = 8
N_COL = 16
MESH = pl.DeviceIdType.MESH
DMA = pltpu.SemaphoreType.DMA
ANY = pl.BlockSpec(memory_space=pl.ANY)


def halves(value):
    high = value.astype(jnp.bfloat16)
    low = (value - high.astype(jnp.float32)).astype(jnp.bfloat16)
    return high, low


def product(left, right, dims=(((1,), (0,)), ((), ()))):
    return lax.dot_general(left, right, dims, preferred_element_type=jnp.float32)


def product3(left, right):
    left_high, left_low = left
    right_high, right_low = right
    return (
        product(left_high, right_high)
        + product(left_high, right_low)
        + product(left_low, right_high)
    )


GROUP = 8


def plan(target_column, first, second):
    for column in range(N_COL):
        first[column] = -1
        second[column] = -1
    for tile in range(target_column.shape[0]):
        column = target_column[tile]
        held = first[column]
        second[column] = jnp.where(held >= 0, tile, -1)
        first[column] = jnp.where(held >= 0, held, tile)


def permute_kernel(target_column, target_tile, tiles, row_map, col_map, out, first, second):
    step = pl.program_id(0)

    @pl.when(step == 0)
    def _():
        plan(target_column, first, second)

    order = lax.broadcasted_iota(jnp.int32, (TILE, TILE), 0)
    across = (((1,), (1,)), ((), ()))

    def place(lane, tile):
        there = jnp.maximum(tile, 0)
        mark = jnp.where(tile >= 0, target_tile[there], -1)
        to_row = (order == row_map[pl.ds(there, 1), :]).astype(jnp.bfloat16)
        to_col = (order == col_map[pl.ds(there, 1), :]).astype(jnp.bfloat16)
        parts = jnp.concatenate(halves(tiles[there]), axis=0)
        moved = product(parts, to_col, across).astype(jnp.bfloat16)
        out[lane, :TILE, :] = product(to_row, moved[:TILE]) + product(to_row, moved[TILE:])
        out[lane, TILE:, :] = jnp.full((8, TILE), mark.astype(jnp.float32))

    for pair in range(GROUP // 2):
        place(2 * pair, first[step * (GROUP // 2) + pair])
    for pair in range(GROUP // 2):
        tile = second[step * (GROUP // 2) + pair]
        out[2 * pair + 1, TILE:, :] = jnp.full((8, TILE), -1.0, jnp.float32)

        @pl.when(tile >= 0)
        def _():
            place(2 * pair + 1, tile)


def permute(target_column, target_tile, tiles, row_map, col_map):
    slots = 2 * N_COL
    count = tiles.shape[0]
    once = pl.Buffered(1)
    return pl.pallas_call(
        permute_kernel,
        out_shape=jax.ShapeDtypeStruct((slots, SLOT, TILE), jnp.float32),
        grid_spec=pltpu.PrefetchScalarGridSpec(
            num_scalar_prefetch=2,
            grid=(slots // GROUP,),
            in_specs=[
                pl.BlockSpec((count, TILE, TILE), lambda s, a, b: (0, 0, 0), pipeline_mode=once),
                pl.BlockSpec((count, TILE), lambda s, a, b: (0, 0), pipeline_mode=once),
                pl.BlockSpec((count, TILE), lambda s, a, b: (0, 0), pipeline_mode=once),
            ],
            out_specs=pl.BlockSpec((GROUP, SLOT, TILE), lambda s, a, b: (s, 0, 0)),
            scratch_shapes=[
                pltpu.SMEM((N_COL,), jnp.int32),
                pltpu.SMEM((N_COL,), jnp.int32),
            ],
        ),
        name="permute",
    )(target_column, target_tile, tiles, row_map, col_map)


NEAR = [(1, 0), (3, 0), (0, 1), (0, 3), (1, 1), (3, 3), (1, 3), (3, 1)]
FAR = [(2, 0), (0, 2), (2, 2), (2, 1), (2, 3), (1, 2), (3, 2)]


def cut(rows, parts):
    edges = [rows // 8 * i // parts * 8 for i in range(parts + 1)]
    return [(edges[i], edges[i + 1] - edges[i]) for i in range(parts)]


def exchange_kernel(sent, got, relay, own_sem, s1, r1, s2, r2, s3, r3):
    row = lax.axis_index("row")
    col = lax.axis_index("col")
    y, x = col // 4, col % 4

    def at(dx, dy):
        return (y + dy) % 4 * 4 + (x + dx) % 4

    peers = [at(dx, dy) for dx, dy in NEAR + FAR]
    barrier = pltpu.get_barrier_semaphore()
    for peer in peers:
        pl.semaphore_signal(barrier, inc=1, device_id=(row, peer), device_id_type=MESH)
    pl.semaphore_wait(barrier, len(peers))

    def remote(source, target, send, receive, device):
        return pltpu.make_async_remote_copy(
            src_ref=source,
            dst_ref=target,
            send_sem=send,
            recv_sem=receive,
            device_id=(row, device),
            device_id_type=MESH,
        )

    own = pltpu.make_async_copy(sent.at[col], got.at[col], own_sem)
    own.start()
    legs = []
    for i, (dx, dy) in enumerate(FAR):
        for half, (first, size) in enumerate(cut(2 * SLOT, 2)):
            step = 1 if half == 0 else 3
            rx, ry = (step if dx == 2 else 0), (step if dy == 2 else 0)
            j = 2 * i + half
            leg = remote(
                sent.at[at(dx, dy), pl.ds(first, size)], relay.at[j], s2.at[j], r2.at[j], at(rx, ry)
            )
            leg.start()
            legs.append((leg, j, at(-rx, -ry), at(dx - rx, dy - ry), first, size))
    straight = []
    for i, (dx, dy) in enumerate(NEAR):
        target = at(dx, dy)
        straight.append(remote(sent.at[target], got.at[col], s1.at[i], r1.at[i], target))
    for copy in straight[:4]:
        copy.start()
    onward = []
    for n, (leg, j, origin, target, first, size) in enumerate(legs):
        leg.wait_recv()
        copy = remote(
            relay.at[j], got.at[origin, pl.ds(first, size)], s3.at[j], r3.at[j], target
        )
        copy.start()
        onward.append(copy)
        if n % 3 == 2 and 4 + n // 3 < len(straight):
            straight[4 + n // 3].start()

    for copy in straight + onward:
        copy.wait()
    for leg, *_ in legs:
        leg.wait_send()
    own.wait()


def exchange(sent):
    return pl.pallas_call(
        exchange_kernel,
        out_shape=jax.ShapeDtypeStruct((N_COL, 2 * SLOT, TILE), jnp.float32),
        in_specs=[ANY],
        out_specs=ANY,
        scratch_shapes=[pltpu.VMEM((2 * len(FAR), SLOT, TILE), jnp.float32), DMA(())]
        + [DMA((len(NEAR),))] * 2
        + [DMA((2 * len(FAR),))] * 4,
        compiler_params=pltpu.CompilerParams(collective_id=1, has_side_effects=True),
        name="exchange",
    )(sent.reshape(N_COL, 2 * SLOT, TILE)).reshape(2 * N_COL, SLOT, TILE)


def assemble_kernel(target, front, got, out, held, sems):
    band = pl.program_id(0)

    def fetch(slot):
        source = got.at[slot, pl.ds(0, TILE)]
        return pltpu.make_async_copy(source, held.at[slot], sems.at[slot])

    @pl.when(band == 0)
    def _():
        for slot in range(target.shape[0]):

            @pl.when(target[slot] >= 0)
            def _():
                fetch(slot).start()

    out[...] = front[...]
    for slot in range(target.shape[0]):
        place = target[slot]

        @pl.when((place >= 0) & (place // 4 == band))
        def _():
            fetch(slot).wait()
            lanes = pl.ds(pl.multiple_of(place % 4 * TILE, TILE), TILE)
            out[:, lanes] += held[slot]


def assemble(front, target, got):
    rows, cols = front.shape
    slots = target.shape[0]
    return pl.pallas_call(
        assemble_kernel,
        out_shape=jax.ShapeDtypeStruct(front.shape, jnp.float32),
        grid_spec=pltpu.PrefetchScalarGridSpec(
            num_scalar_prefetch=1,
            grid=(rows // TILE,),
            in_specs=[pl.BlockSpec((TILE, cols), lambda i, t: (i, 0))] + [ANY],
            out_specs=pl.BlockSpec((TILE, cols), lambda i, t: (i, 0)),
            scratch_shapes=[pltpu.VMEM((slots, TILE, TILE), jnp.float32), DMA((slots,))],
        ),
        name="assemble",
    )(target, front, got)


PIECE = 16
PIECES = 32
BAND = 16
BANDS = 16
HOP = 3
CORNER_AT = 23
CORNER_HOP = 6


def spanning_trees():
    trees = []
    for tree in range(4):
        depth, edges = {}, []

        def grow(node, last, level):
            depth[node] = level
            for turn in range(last + 1, 4):
                bit = ((turn + 1) % 4 + tree) % 4
                child = node ^ (1 << bit)
                if child != 0:
                    edges.append((node, bit))
                    grow(child, turn, level + 1)

        grow(1 << tree, -1, 1)
        edges.append((0, tree))
        trees.append((depth, edges))
    return trees


def gray(column):
    y, x = column // 4, column % 4
    return (x ^ (x >> 1)) + 4 * (y ^ (y >> 1))


def panel_kernel(front, block, band, corner, ts, tr, cs, cr, us, ur, qs, qr, vs, vr, ws, wr):
    row = lax.axis_index("row")
    col = lax.axis_index("col")
    y, x = col // 4, col % 4
    z, core = row // 2, row % 2
    beside = [
        (row, y * 4 + (x + 1 - 2 * (x % 2))),
        (row, y * 4 + 3 - x),
        (row, (y + 1 - 2 * (y % 2)) * 4 + x),
        (row, (3 - y) * 4 + x),
    ]
    along = [((z + 1) % 4 * 2 + core, col), ((z + 3) % 4 * 2 + core, col)]
    partner = (z * 2 + 1 - core, col)
    barrier = pltpu.get_barrier_semaphore()
    for device in beside + along + [partner]:
        pl.semaphore_signal(barrier, inc=1, device_id=device, device_id_type=MESH)
    pl.semaphore_wait(barrier, 7)

    trees = spanning_trees()
    names = {gray(column): column for column in range(N_COL)}
    level, sends = [], []
    for depth, edges in trees:
        at = jnp.int32(0)
        for node, steps in depth.items():
            at = at + jnp.where(col == names[node], steps, 0)
        level.append(at)
        by_bit = {}
        for bit in range(4):
            nodes = [names[node] for node, b in edges if b == bit and node != 0]
            if nodes:
                by_bit[bit] = functools.reduce(jnp.logical_or, [col == node for node in nodes])
        sends.append(by_bit)
    root = col == 0
    upper = row == 0
    leads = core == 0
    way = [z, (4 - z) % 4]

    def remote(source, target, send, receive, device):
        return pltpu.make_async_remote_copy(
            src_ref=source,
            dst_ref=target,
            send_sem=send,
            recv_sem=receive,
            device_id=device,
            device_id_type=MESH,
        )

    def block_piece(tree, piece):
        return block.at[pl.ds(pl.multiple_of((piece * 4 + tree) * PIECE, PIECE), PIECE)]

    def block_copy(tree, bit, piece, source):
        return remote(
            source, block_piece(tree, piece), ts.at[tree, bit], tr.at[tree, piece], beside[bit]
        )

    def corner_copy(tree, bit, source):
        target = corner.at[pl.ds(tree * 64, 64)]
        return remote(source, target, cs.at[tree, bit], cr.at[tree], beside[bit])

    def front_piece(tree, piece):
        first = pl.multiple_of((piece * 4 + tree) * PIECE, PIECE)
        return front.at[pl.ds(first, PIECE), pl.ds(0, 2 * TILE)]

    def band_piece(ref, half, piece):
        return ref.at[pl.ds(pl.multiple_of(half * TILE + piece * BAND, BAND), BAND)]

    def corner_half(half):
        return corner.at[pl.ds(half * TILE, TILE)]

    def step(now, carry):
        for tree in range(4):
            piece = now - HOP * level[tree] - 1

            @pl.when((piece == -1) & upper)
            def _():
                @pl.when(root)
                def _():
                    source = front.at[pl.ds(tree * 64, 64), pl.ds(TILE, TILE)]
                    corner_copy(tree, tree, source).start()

                @pl.when(jnp.logical_not(root))
                def _():
                    source = corner.at[pl.ds(tree * 64, 64)]
                    corner_copy(tree, 0, source).wait_recv()
                    for bit, here in sends[tree].items():

                        @pl.when(here)
                        def _():
                            corner_copy(tree, bit, source).start()

            @pl.when((piece >= 0) & (piece < PIECES))
            def _():
                @pl.when(root)
                def _():
                    block_copy(tree, tree, piece, front_piece(tree, piece)).start()

                @pl.when(jnp.logical_not(root))
                def _():
                    source = block_piece(tree, piece)
                    block_copy(tree, 0, piece, source).wait_recv()
                    for bit, here in sends[tree].items():

                        @pl.when(here)
                        def _():
                            block_copy(tree, bit, piece, source).start()

        for half in range(2):
            hops = way[half]
            piece = now - HOP * hops

            def band_copy(source, which):
                target = band_piece(band, half, piece)
                if which == 0:
                    return remote(source, target, us.at[half], ur.at[half, piece], along[half])
                return remote(source, target, qs.at[half], qr.at[half], partner)

            @pl.when(leads & (piece >= 0) & (piece < BANDS))
            def _():
                @pl.when(hops == 0)
                def _():
                    source = band_piece(front, half, piece)
                    band_copy(source, 0).start()
                    band_copy(source, 1).start()

                @pl.when(hops > 0)
                def _():
                    source = band_piece(band, half, piece)
                    band_copy(source, 0).wait_recv()

                    @pl.when(hops < 3)
                    def _():
                        band_copy(source, 0).start()

                    band_copy(source, 1).start()

            def pass_on(source):
                @pl.when(hops < 3)
                def _():
                    remote(source, corner_half(half), vs.at[half], vr.at[half], along[half]).start()

                remote(source, corner_half(half), ws.at[half], wr.at[half], partner).start()

            @pl.when(leads & (now == CORNER_AT + CORNER_HOP * hops))
            def _():
                @pl.when(upper & root)
                def _():
                    if half == 0:
                        pass_on(front.at[pl.ds(0, TILE), pl.ds(TILE, TILE)])
                    else:
                        pass_on(front.at[pl.ds(TILE, TILE), pl.ds(0, TILE)])

                @pl.when(upper & jnp.logical_not(root))
                def _():
                    if half == 0:
                        pass_on(corner_half(0))
                    else:
                        pass_on(block.at[pl.ds(TILE, TILE), pl.ds(0, TILE)])

                @pl.when(jnp.logical_not(upper))
                def _():
                    source = corner_half(half)
                    remote(source, source, vs.at[half], vr.at[half], along[half]).wait_recv()
                    pass_on(source)

        return carry

    lax.fori_loop(0, PIECES + 1 + 5 * HOP, step, 0)

    whole = block.at[pl.ds(0, PIECE * PIECES)]
    for tree in range(4):

        def sent(bit):
            remote(whole, whole, ts.at[tree, bit], tr.at[tree, 0], beside[bit]).wait_send()

            @pl.when(upper)
            def _():
                corner_copy(tree, bit, corner.at[pl.ds(tree * 64, 64)]).wait_send()

        @pl.when(root)
        def _():
            sent(tree)

        for bit, here in sends[tree].items():

            @pl.when(here)
            def _():
                sent(bit)

    for half in range(2):
        whole_band = band.at[pl.ds(half * TILE, TILE)]
        band_along = remote(whole_band, whole_band, us.at[half], ur.at[half, 0], along[half])
        band_beside = remote(whole_band, whole_band, qs.at[half], qr.at[half], partner)
        ends = corner_half(half)
        corner_along = remote(ends, ends, vs.at[half], vr.at[half], along[half])
        corner_beside = remote(ends, ends, ws.at[half], wr.at[half], partner)

        @pl.when(leads)
        def _():
            @pl.when(way[half] < 3)
            def _():
                band_along.wait_send()
                corner_along.wait_send()

            band_beside.wait_send()
            corner_beside.wait_send()

        @pl.when(jnp.logical_not(leads))
        def _():
            band_beside.wait_recv()
            corner_beside.wait_recv()


def share_panels(front):
    rows, cols = front.shape
    return pl.pallas_call(
        panel_kernel,
        out_shape=(
            jax.ShapeDtypeStruct((rows, 2 * TILE), jnp.float32),
            jax.ShapeDtypeStruct((2 * TILE, cols), jnp.float32),
            jax.ShapeDtypeStruct((2 * TILE, TILE), jnp.float32),
        ),
        in_specs=[ANY],
        out_specs=(ANY,) * 3,
        scratch_shapes=[
            DMA((4, 4)),
            DMA((4, PIECES)),
            DMA((4, 4)),
            DMA((4,)),
            DMA((2,)),
            DMA((2, BANDS)),
        ]
        + [DMA((2,))] * 6,
        compiler_params=pltpu.CompilerParams(collective_id=2, has_side_effects=True),
        name="share_panels",
    )(front)


def update_kernel(
    front, block, band, corner, top, side, inverse, out,
    up_high, up_low, near_high, near_low, mix_high, mix_low,
):
    step = pl.program_id(0)
    row = lax.axis_index("row")
    root = lax.axis_index("col") == 0
    upper = row == 0
    number = row * pl.num_programs(0) + step

    @pl.when(step == 0)
    def _():
        band_now = jnp.where(upper, top[...], band[...])
        right = jnp.where(upper & root, top[:TILE, TILE : 2 * TILE], corner[:TILE])
        below = jnp.where(root, top[TILE:, :TILE], side[...])
        below = jnp.where(upper, below, corner[TILE:])
        inverse_0, inverse_1 = halves(inverse[0]), halves(inverse[1])
        first = halves(band_now[:TILE])
        ahead = product3(inverse_0, first)
        cross = product3(halves(below), halves(ahead))
        second = halves(band_now[TILE:] - cross)
        mixed = product3(halves(right), inverse_1)
        mixed = product3(inverse_0, halves(mixed))
        mix = halves(mixed)
        near_high[...], near_low[...] = halves(ahead)
        up_high[:TILE], up_low[:TILE] = halves(ahead - product3(mix, second))
        up_high[TILE:], up_low[TILE:] = halves(product3(inverse_1, second))
        for place, parts in enumerate((inverse_0, inverse_1, mix)):
            mix_high[place], mix_low[place] = parts

    @pl.when(number == 0)
    def _():
        out[...] = front[...]

    @pl.when((number > 0) & jnp.logical_not(root))
    def _():
        high, low = halves(block[...])

        @pl.when(number > 1)
        def _():
            out[...] = front[...] - product3((high, low), (up_high[...], up_low[...]))

        @pl.when(number == 1)
        def _():
            left = high[:, :TILE], low[:, :TILE]
            out[...] = front[...] - product3(left, (near_high[...], near_low[...]))

    @pl.when((number > 0) & root)
    def _():
        high, low = halves(front[:, : 2 * TILE])
        left, right = (high[:, :TILE], low[:, :TILE]), (high[:, TILE:], low[:, TILE:])
        out[:, :TILE] = product3(left, (mix_high[0], mix_low[0]))

        @pl.when(number > 1)
        def _():
            lower = product3(right, (mix_high[1], mix_low[1]))
            out[:, TILE : 2 * TILE] = lower - product3(left, (mix_high[2], mix_low[2]))
            parts = up_high[:, 2 * TILE :], up_low[:, 2 * TILE :]
            out[:, 2 * TILE :] = front[:, 2 * TILE :] - product3((high, low), parts)

        @pl.when(number == 1)
        def _():
            parts = near_high[:, TILE:], near_low[:, TILE:]
            out[:, TILE:] = front[:, TILE:] - product3(left, parts)


def update(front, block, band, corner, inverse):
    rows, cols = front.shape
    once = pl.Buffered(1)
    return pl.pallas_call(
        update_kernel,
        out_shape=jax.ShapeDtypeStruct(front.shape, jnp.float32),
        grid=(rows // TILE,),
        in_specs=[
            pl.BlockSpec((TILE, cols), lambda i: (i, 0)),
            pl.BlockSpec((TILE, 2 * TILE), lambda i: (i, 0)),
            pl.BlockSpec((2 * TILE, cols), lambda i: (0, 0), pipeline_mode=once),
            pl.BlockSpec((2 * TILE, TILE), lambda i: (0, 0), pipeline_mode=once),
            pl.BlockSpec((2 * TILE, cols), lambda i: (0, 0), pipeline_mode=once),
            pl.BlockSpec((TILE, TILE), lambda i: (1, 0), pipeline_mode=once),
            pl.BlockSpec((2, TILE, TILE), lambda i: (0, 0, 0), pipeline_mode=once),
        ],
        out_specs=pl.BlockSpec((TILE, cols), lambda i: (i, 0)),
        scratch_shapes=[pltpu.VMEM((2 * TILE, cols), jnp.bfloat16)] * 2
        + [pltpu.VMEM((TILE, cols), jnp.bfloat16)] * 2
        + [pltpu.VMEM((3, TILE, TILE), jnp.bfloat16)] * 2,
        name="update",
    )(front, block, band, corner, front, block, inverse)


def per_device(
    front_matrix, child_tiles, target_column, target_tile, row_map, col_map, pivot_inverse
):
    count = child_tiles.shape[2]
    rows = front_matrix.shape[0]
    routed = (
        target_column.reshape(count),
        target_tile.reshape(count),
        child_tiles.reshape(count, TILE, TILE),
        row_map.reshape(count, TILE),
        col_map.reshape(count, TILE),
    )
    got = exchange(permute(*routed))
    front = assemble(front_matrix, got[:, TILE, 0].astype(jnp.int32), got)
    block, band, corner = share_panels(front)
    return update(front, block, band, corner, pivot_inverse)


def solution(mesh):
    in_specs = (
        P("row", "col"),
        P("row", "col", None, None, None),
        P("row", "col", None, None),
        P("row", "col", None),
        P("row", "col", None, None),
        P("row", "col", None, None),
        P(),
    )
    return jax.shard_map(
        per_device, mesh=mesh, in_specs=in_specs, out_specs=P("row", "col"), check_vma=False
    )
```

```python
import functools
import jax
import jax.numpy as jnp
from jax import lax
from jax.experimental import pallas as pl
from jax.experimental.pallas import tpu as pltpu
from jax.sharding import PartitionSpec as P

TILE = 256
SLOT = TILE + 8
N_ROW = 8
N_COL = 16
MESH = pl.DeviceIdType.MESH
DMA = pltpu.SemaphoreType.DMA
ANY = pl.BlockSpec(memory_space=pl.ANY)


def halves(value):
    high = value.astype(jnp.bfloat16)
    low = (value - high.astype(jnp.float32)).astype(jnp.bfloat16)
    return high, low


def product(left, right, dims=(((1,), (0,)), ((), ()))):
    return lax.dot_general(left, right, dims, preferred_element_type=jnp.float32)


def product3(left, right):
    left_high, left_low = left
    right_high, right_low = right
    return (
        product(left_high, right_high)
        + product(left_high, right_low)
        + product(left_low, right_high)
    )


GROUP = 8


def plan(target_column, first, second):
    for column in range(N_COL):
        first[column] = -1
        second[column] = -1
    for tile in range(target_column.shape[0]):
        column = target_column[tile]
        held = first[column]
        second[column] = jnp.where(held >= 0, tile, -1)
        first[column] = jnp.where(held >= 0, held, tile)


def permute_kernel(target_column, target_tile, tiles, row_map, col_map, out, first, second):
    step = pl.program_id(0)

    @pl.when(step == 0)
    def _():
        plan(target_column, first, second)

    order = lax.broadcasted_iota(jnp.int32, (TILE, TILE), 0)
    across = (((1,), (1,)), ((), ()))

    def place(lane, tile):
        there = jnp.maximum(tile, 0)
        mark = jnp.where(tile >= 0, target_tile[there], -1)
        to_row = (order == row_map[pl.ds(there, 1), :]).astype(jnp.bfloat16)
        to_col = (order == col_map[pl.ds(there, 1), :]).astype(jnp.bfloat16)
        parts = jnp.concatenate(halves(tiles[there]), axis=0)
        moved = product(parts, to_col, across).astype(jnp.bfloat16)
        out[lane, :TILE, :] = product(to_row, moved[:TILE]) + product(to_row, moved[TILE:])
        out[lane, TILE:, :] = jnp.full((8, TILE), mark.astype(jnp.float32))

    for pair in range(GROUP // 2):
        place(2 * pair, first[step * (GROUP // 2) + pair])
    for pair in range(GROUP // 2):
        tile = second[step * (GROUP // 2) + pair]
        out[2 * pair + 1, TILE:, :] = jnp.full((8, TILE), -1.0, jnp.float32)

        @pl.when(tile >= 0)
        def _():
            place(2 * pair + 1, tile)


def permute(target_column, target_tile, tiles, row_map, col_map):
    slots = 2 * N_COL
    count = tiles.shape[0]
    once = pl.Buffered(1)
    return pl.pallas_call(
        permute_kernel,
        out_shape=jax.ShapeDtypeStruct((slots, SLOT, TILE), jnp.float32),
        grid_spec=pltpu.PrefetchScalarGridSpec(
            num_scalar_prefetch=2,
            grid=(slots // GROUP,),
            in_specs=[
                pl.BlockSpec((count, TILE, TILE), lambda s, a, b: (0, 0, 0), pipeline_mode=once),
                pl.BlockSpec((count, TILE), lambda s, a, b: (0, 0), pipeline_mode=once),
                pl.BlockSpec((count, TILE), lambda s, a, b: (0, 0), pipeline_mode=once),
            ],
            out_specs=pl.BlockSpec((GROUP, SLOT, TILE), lambda s, a, b: (s, 0, 0)),
            scratch_shapes=[
                pltpu.SMEM((N_COL,), jnp.int32),
                pltpu.SMEM((N_COL,), jnp.int32),
            ],
        ),
        name="permute",
    )(target_column, target_tile, tiles, row_map, col_map)


NEAR = [(1, 0), (3, 0), (0, 1), (0, 3), (1, 1), (3, 3), (1, 3), (3, 1)]
FAR = [(2, 0), (0, 2), (2, 2), (2, 1), (2, 3), (1, 2), (3, 2)]


def cut(rows, parts):
    edges = [rows // 8 * i // parts * 8 for i in range(parts + 1)]
    return [(edges[i], edges[i + 1] - edges[i]) for i in range(parts)]


def exchange_kernel(sent, got, relay, own_sem, s1, r1, s2, r2, s3, r3):
    row = lax.axis_index("row")
    col = lax.axis_index("col")
    y, x = col // 4, col % 4

    def at(dx, dy):
        return (y + dy) % 4 * 4 + (x + dx) % 4

    peers = [at(dx, dy) for dx, dy in NEAR + FAR]
    barrier = pltpu.get_barrier_semaphore()
    for peer in peers:
        pl.semaphore_signal(barrier, inc=1, device_id=(row, peer), device_id_type=MESH)
    pl.semaphore_wait(barrier, len(peers))

    def remote(source, target, send, receive, device):
        return pltpu.make_async_remote_copy(
            src_ref=source,
            dst_ref=target,
            send_sem=send,
            recv_sem=receive,
            device_id=(row, device),
            device_id_type=MESH,
        )

    own = pltpu.make_async_copy(sent.at[col], got.at[col], own_sem)
    own.start()
    legs = []
    for i, (dx, dy) in enumerate(FAR):
        for half, (first, size) in enumerate(cut(2 * SLOT, 2)):
            step = 1 if half == 0 else 3
            rx, ry = (step if dx == 2 else 0), (step if dy == 2 else 0)
            j = 2 * i + half
            leg = remote(
                sent.at[at(dx, dy), pl.ds(first, size)], relay.at[j], s2.at[j], r2.at[j], at(rx, ry)
            )
            leg.start()
            legs.append((leg, j, at(-rx, -ry), at(dx - rx, dy - ry), first, size))
    straight = []
    for i, (dx, dy) in enumerate(NEAR):
        target = at(dx, dy)
        straight.append(remote(sent.at[target], got.at[col], s1.at[i], r1.at[i], target))
    for copy in straight[:4]:
        copy.start()
    onward = []
    for n, (leg, j, origin, target, first, size) in enumerate(legs):
        leg.wait_recv()
        copy = remote(
            relay.at[j], got.at[origin, pl.ds(first, size)], s3.at[j], r3.at[j], target
        )
        copy.start()
        onward.append(copy)
        if n % 3 == 2 and 4 + n // 3 < len(straight):
            straight[4 + n // 3].start()

    for copy in straight + onward:
        copy.wait()
    for leg, *_ in legs:
        leg.wait_send()
    own.wait()


def exchange(sent):
    return pl.pallas_call(
        exchange_kernel,
        out_shape=jax.ShapeDtypeStruct((N_COL, 2 * SLOT, TILE), jnp.float32),
        in_specs=[ANY],
        out_specs=ANY,
        scratch_shapes=[pltpu.VMEM((2 * len(FAR), SLOT, TILE), jnp.float32), DMA(())]
        + [DMA((len(NEAR),))] * 2
        + [DMA((2 * len(FAR),))] * 4,
        compiler_params=pltpu.CompilerParams(collective_id=1, has_side_effects=True),
        name="exchange",
    )(sent.reshape(N_COL, 2 * SLOT, TILE)).reshape(2 * N_COL, SLOT, TILE)


def assemble_kernel(target, front, got, out, held, sems):
    band = pl.program_id(0)

    def fetch(slot):
        source = got.at[slot, pl.ds(0, TILE)]
        return pltpu.make_async_copy(source, held.at[slot], sems.at[slot])

    @pl.when(band == 0)
    def _():
        for slot in range(target.shape[0]):

            @pl.when(target[slot] >= 0)
            def _():
                fetch(slot).start()

    out[...] = front[...]
    for slot in range(target.shape[0]):
        place = target[slot]

        @pl.when((place >= 0) & (place // 4 == band))
        def _():
            fetch(slot).wait()
            lanes = pl.ds(pl.multiple_of(place % 4 * TILE, TILE), TILE)
            out[:, lanes] += held[slot]


def assemble(front, target, got):
    rows, cols = front.shape
    slots = target.shape[0]
    return pl.pallas_call(
        assemble_kernel,
        out_shape=jax.ShapeDtypeStruct(front.shape, jnp.float32),
        grid_spec=pltpu.PrefetchScalarGridSpec(
            num_scalar_prefetch=1,
            grid=(rows // TILE,),
            in_specs=[pl.BlockSpec((TILE, cols), lambda i, t: (i, 0))] + [ANY],
            out_specs=pl.BlockSpec((TILE, cols), lambda i, t: (i, 0)),
            scratch_shapes=[pltpu.VMEM((slots, TILE, TILE), jnp.float32), DMA((slots,))],
        ),
        name="assemble",
    )(target, front, got)


PIECE = 32
PIECES = 16
BAND = 16
BANDS = 16
HOP = 3
CORNER_AT = 19
CORNER_HOP = 4


def spanning_trees():
    trees = []
    for tree in range(4):
        depth, edges = {}, []

        def grow(node, last, level):
            depth[node] = level
            for turn in range(last + 1, 4):
                bit = ((turn + 1) % 4 + tree) % 4
                child = node ^ (1 << bit)
                if child != 0:
                    edges.append((node, bit))
                    grow(child, turn, level + 1)

        grow(1 << tree, -1, 1)
        edges.append((0, tree))
        trees.append((depth, edges))
    return trees


def gray(column):
    y, x = column // 4, column % 4
    return (x ^ (x >> 1)) + 4 * (y ^ (y >> 1))


def panel_kernel(front, block, band, corner, ts, tr, cs, cr, us, ur, qs, qr, vs, vr, ws, wr):
    row = lax.axis_index("row")
    col = lax.axis_index("col")
    y, x = col // 4, col % 4
    z, core = row // 2, row % 2
    beside = [
        (row, y * 4 + (x + 1 - 2 * (x % 2))),
        (row, y * 4 + 3 - x),
        (row, (y + 1 - 2 * (y % 2)) * 4 + x),
        (row, (3 - y) * 4 + x),
    ]
    along = [((z + 1) % 4 * 2 + core, col), ((z + 3) % 4 * 2 + core, col)]
    partner = (z * 2 + 1 - core, col)
    barrier = pltpu.get_barrier_semaphore()
    for device in beside + along + [partner]:
        pl.semaphore_signal(barrier, inc=1, device_id=device, device_id_type=MESH)
    pl.semaphore_wait(barrier, 7)

    trees = spanning_trees()
    names = {gray(column): column for column in range(N_COL)}
    level, sends = [], []
    for depth, edges in trees:
        at = jnp.int32(0)
        for node, steps in depth.items():
            at = at + jnp.where(col == names[node], steps, 0)
        level.append(at)
        by_bit = {}
        for bit in range(4):
            nodes = [names[node] for node, b in edges if b == bit and node != 0]
            if nodes:
                by_bit[bit] = functools.reduce(jnp.logical_or, [col == node for node in nodes])
        sends.append(by_bit)
    root = col == 0
    upper = row == 0
    leads = core == 0
    way = [z, (4 - z) % 4]

    def remote(source, target, send, receive, device):
        return pltpu.make_async_remote_copy(
            src_ref=source,
            dst_ref=target,
            send_sem=send,
            recv_sem=receive,
            device_id=device,
            device_id_type=MESH,
        )

    def block_piece(tree, piece):
        return block.at[pl.ds(pl.multiple_of((piece * 4 + tree) * PIECE, PIECE), PIECE)]

    def block_copy(tree, bit, piece, source):
        return remote(
            source, block_piece(tree, piece), ts.at[tree, bit], tr.at[tree, piece], beside[bit]
        )

    def corner_copy(tree, bit, source):
        target = corner.at[pl.ds(tree * 64, 64)]
        return remote(source, target, cs.at[tree, bit], cr.at[tree], beside[bit])

    def front_piece(tree, piece):
        first = pl.multiple_of((piece * 4 + tree) * PIECE, PIECE)
        return front.at[pl.ds(first, PIECE), pl.ds(0, 2 * TILE)]

    def band_piece(ref, half, piece):
        return ref.at[pl.ds(pl.multiple_of(half * TILE + piece * BAND, BAND), BAND)]

    def corner_half(half):
        return corner.at[pl.ds(half * TILE, TILE)]

    def step(now, carry):
        for tree in range(4):
            piece = now - HOP * level[tree] - 1

            @pl.when((piece == -1) & upper)
            def _():
                @pl.when(root)
                def _():
                    source = front.at[pl.ds(tree * 64, 64), pl.ds(TILE, TILE)]
                    corner_copy(tree, tree, source).start()

                @pl.when(jnp.logical_not(root))
                def _():
                    source = corner.at[pl.ds(tree * 64, 64)]
                    corner_copy(tree, 0, source).wait_recv()
                    for bit, here in sends[tree].items():

                        @pl.when(here)
                        def _():
                            corner_copy(tree, bit, source).start()

            @pl.when((piece >= 0) & (piece < PIECES))
            def _():
                @pl.when(root)
                def _():
                    block_copy(tree, tree, piece, front_piece(tree, piece)).start()

                @pl.when(jnp.logical_not(root))
                def _():
                    source = block_piece(tree, piece)
                    block_copy(tree, 0, piece, source).wait_recv()
                    for bit, here in sends[tree].items():

                        @pl.when(here)
                        def _():
                            block_copy(tree, bit, piece, source).start()

        for half in range(2):
            hops = way[half]
            piece = now - HOP * hops

            def band_copy(source, which):
                target = band_piece(band, half, piece)
                if which == 0:
                    return remote(source, target, us.at[half], ur.at[half, piece], along[half])
                return remote(source, target, qs.at[half], qr.at[half], partner)

            @pl.when(leads & (piece >= 0) & (piece < BANDS))
            def _():
                @pl.when(hops == 0)
                def _():
                    source = band_piece(front, half, piece)
                    band_copy(source, 0).start()
                    band_copy(source, 1).start()

                @pl.when(hops > 0)
                def _():
                    source = band_piece(band, half, piece)
                    band_copy(source, 0).wait_recv()

                    @pl.when(hops < 3)
                    def _():
                        band_copy(source, 0).start()

                    band_copy(source, 1).start()

            def pass_on(source):
                @pl.when(hops < 3)
                def _():
                    remote(source, corner_half(half), vs.at[half], vr.at[half], along[half]).start()

                remote(source, corner_half(half), ws.at[half], wr.at[half], partner).start()

            @pl.when(leads & (now == CORNER_AT + CORNER_HOP * hops))
            def _():
                @pl.when(upper & root)
                def _():
                    if half == 0:
                        pass_on(front.at[pl.ds(0, TILE), pl.ds(TILE, TILE)])
                    else:
                        pass_on(front.at[pl.ds(TILE, TILE), pl.ds(0, TILE)])

                @pl.when(upper & jnp.logical_not(root))
                def _():
                    if half == 0:
                        pass_on(corner_half(0))
                    else:
                        pass_on(block.at[pl.ds(TILE, TILE), pl.ds(0, TILE)])

                @pl.when(jnp.logical_not(upper))
                def _():
                    source = corner_half(half)
                    remote(source, source, vs.at[half], vr.at[half], along[half]).wait_recv()
                    pass_on(source)

        return carry

    lax.fori_loop(0, PIECES + 1 + 5 * HOP, step, 0)

    whole = block.at[pl.ds(0, PIECE * PIECES)]
    for tree in range(4):

        def sent(bit):
            remote(whole, whole, ts.at[tree, bit], tr.at[tree, 0], beside[bit]).wait_send()

            @pl.when(upper)
            def _():
                corner_copy(tree, bit, corner.at[pl.ds(tree * 64, 64)]).wait_send()

        @pl.when(root)
        def _():
            sent(tree)

        for bit, here in sends[tree].items():

            @pl.when(here)
            def _():
                sent(bit)

    for half in range(2):
        whole_band = band.at[pl.ds(half * TILE, TILE)]
        band_along = remote(whole_band, whole_band, us.at[half], ur.at[half, 0], along[half])
        band_beside = remote(whole_band, whole_band, qs.at[half], qr.at[half], partner)
        ends = corner_half(half)
        corner_along = remote(ends, ends, vs.at[half], vr.at[half], along[half])
        corner_beside = remote(ends, ends, ws.at[half], wr.at[half], partner)

        @pl.when(leads)
        def _():
            @pl.when(way[half] < 3)
            def _():
                band_along.wait_send()
                corner_along.wait_send()

            band_beside.wait_send()
            corner_beside.wait_send()

        @pl.when(jnp.logical_not(leads))
        def _():
            band_beside.wait_recv()
            corner_beside.wait_recv()


def share_panels(front):
    rows, cols = front.shape
    return pl.pallas_call(
        panel_kernel,
        out_shape=(
            jax.ShapeDtypeStruct((rows, 2 * TILE), jnp.float32),
            jax.ShapeDtypeStruct((2 * TILE, cols), jnp.float32),
            jax.ShapeDtypeStruct((2 * TILE, TILE), jnp.float32),
        ),
        in_specs=[ANY],
        out_specs=(ANY,) * 3,
        scratch_shapes=[
            DMA((4, 4)),
            DMA((4, PIECES)),
            DMA((4, 4)),
            DMA((4,)),
            DMA((2,)),
            DMA((2, BANDS)),
        ]
        + [DMA((2,))] * 6,
        compiler_params=pltpu.CompilerParams(collective_id=2, has_side_effects=True),
        name="share_panels",
    )(front)


def update_kernel(
    front, block, band, corner, top, side, inverse, out,
    up_high, up_low, near_high, near_low, mix_high, mix_low,
):
    step = pl.program_id(0)
    row = lax.axis_index("row")
    root = lax.axis_index("col") == 0
    upper = row == 0
    number = row * pl.num_programs(0) + step

    @pl.when(step == 0)
    def _():
        band_now = jnp.where(upper, top[...], band[...])
        right = jnp.where(upper & root, top[:TILE, TILE : 2 * TILE], corner[:TILE])
        below = jnp.where(root, top[TILE:, :TILE], side[...])
        below = jnp.where(upper, below, corner[TILE:])
        inverse_0, inverse_1 = halves(inverse[0]), halves(inverse[1])
        first = halves(band_now[:TILE])
        ahead = product3(inverse_0, first)
        cross = product3(halves(below), halves(ahead))
        second = halves(band_now[TILE:] - cross)
        mixed = product3(halves(right), inverse_1)
        mixed = product3(inverse_0, halves(mixed))
        mix = halves(mixed)
        near_high[...], near_low[...] = halves(ahead)
        up_high[:TILE], up_low[:TILE] = halves(ahead - product3(mix, second))
        up_high[TILE:], up_low[TILE:] = halves(product3(inverse_1, second))
        for place, parts in enumerate((inverse_0, inverse_1, mix)):
            mix_high[place], mix_low[place] = parts

    @pl.when(number == 0)
    def _():
        out[...] = front[...]

    @pl.when((number > 0) & jnp.logical_not(root))
    def _():
        high, low = halves(block[...])

        @pl.when(number > 1)
        def _():
            out[...] = front[...] - product3((high, low), (up_high[...], up_low[...]))

        @pl.when(number == 1)
        def _():
            left = high[:, :TILE], low[:, :TILE]
            out[...] = front[...] - product3(left, (near_high[...], near_low[...]))

    @pl.when((number > 0) & root)
    def _():
        high, low = halves(front[:, : 2 * TILE])
        left, right = (high[:, :TILE], low[:, :TILE]), (high[:, TILE:], low[:, TILE:])
        out[:, :TILE] = product3(left, (mix_high[0], mix_low[0]))

        @pl.when(number > 1)
        def _():
            lower = product3(right, (mix_high[1], mix_low[1]))
            out[:, TILE : 2 * TILE] = lower - product3(left, (mix_high[2], mix_low[2]))
            parts = up_high[:, 2 * TILE :], up_low[:, 2 * TILE :]
            out[:, 2 * TILE :] = front[:, 2 * TILE :] - product3((high, low), parts)

        @pl.when(number == 1)
        def _():
            parts = near_high[:, TILE:], near_low[:, TILE:]
            out[:, TILE:] = front[:, TILE:] - product3(left, parts)


def update(front, block, band, corner, inverse):
    rows, cols = front.shape
    once = pl.Buffered(1)
    return pl.pallas_call(
        update_kernel,
        out_shape=jax.ShapeDtypeStruct(front.shape, jnp.float32),
        grid=(rows // TILE,),
        in_specs=[
            pl.BlockSpec((TILE, cols), lambda i: (i, 0)),
            pl.BlockSpec((TILE, 2 * TILE), lambda i: (i, 0)),
            pl.BlockSpec((2 * TILE, cols), lambda i: (0, 0), pipeline_mode=once),
            pl.BlockSpec((2 * TILE, TILE), lambda i: (0, 0), pipeline_mode=once),
            pl.BlockSpec((2 * TILE, cols), lambda i: (0, 0), pipeline_mode=once),
            pl.BlockSpec((TILE, TILE), lambda i: (1, 0), pipeline_mode=once),
            pl.BlockSpec((2, TILE, TILE), lambda i: (0, 0, 0), pipeline_mode=once),
        ],
        out_specs=pl.BlockSpec((TILE, cols), lambda i: (i, 0)),
        scratch_shapes=[pltpu.VMEM((2 * TILE, cols), jnp.bfloat16)] * 2
        + [pltpu.VMEM((TILE, cols), jnp.bfloat16)] * 2
        + [pltpu.VMEM((3, TILE, TILE), jnp.bfloat16)] * 2,
        name="update",
    )(front, block, band, corner, front, block, inverse)


def per_device(
    front_matrix, child_tiles, target_column, target_tile, row_map, col_map, pivot_inverse
):
    count = child_tiles.shape[2]
    rows = front_matrix.shape[0]
    routed = (
        target_column.reshape(count),
        target_tile.reshape(count),
        child_tiles.reshape(count, TILE, TILE),
        row_map.reshape(count, TILE),
        col_map.reshape(count, TILE),
    )
    got = exchange(permute(*routed))
    front = assemble(front_matrix, got[:, TILE, 0].astype(jnp.int32), got)
    block, band, corner = share_panels(front)
    return update(front, block, band, corner, pivot_inverse)


def solution(mesh):
    in_specs = (
        P("row", "col"),
        P("row", "col", None, None, None),
        P("row", "col", None, None),
        P("row", "col", None),
        P("row", "col", None, None),
        P("row", "col", None, None),
        P(),
    )
    return jax.shard_map(
        per_device, mesh=mesh, in_specs=in_specs, out_specs=P("row", "col"), check_vma=False
    )
```
